32 devices in a mesh: ctx: 8 (over z, core), tp: 4 (over y, x).
Axes of the slice: x: 2, y: 2, z: 4, core: 2. Of those that a mesh axis runs over, the one named last changes fastest.
Arguments:
- tokens: bfloat16 [4096, 8192], P(('ctx', 'tp')), may hold values from -6 to 6
- norm_gain: float32 [8192], replicated, may hold values from 0.1 to 1.9
- w_query: bfloat16 [8192, 4096], P(None, 'tp'), may hold values from -1 to 1
- query_scale: float32 [64, 32], P(None, 'tp'), may hold values from 0.5 to 2
- w_key: bfloat16 [8192, 1024], P(None, 'tp'), may hold values from -1 to 1
- key_scale: float32 [64, 8], P(None, 'tp'), may hold values from 0.5 to 2
- w_value: bfloat16 [8192, 1024], P(None, 'tp'), may hold values from -0.0625 to 0.0625
- value_scale: float32 [64, 8], P(None, 'tp'), may hold values from 0.5 to 2
- w_out: bfloat16 [4096, 8192], P('tp'), may hold values from -0.09375 to 0.09375
- out_scale: float32 [32, 64], P('tp'), may hold values from 0.5 to 2
- score_vec: bfloat16 [8192], replicated, may hold values from -0.0625 to 0.0625
- doc_ids: int32 [4096], replicated, may hold values from 0 to 3, never falling along the last dimension, each value on 1 to 1280 neighbouring positions
- span_of: int32 [8], replicated, may hold values from 0 to 7, each once
Outputs:
- hidden: bfloat16 [4096, 8192], P(('ctx', 'tp'))
- doc_score: float32 [4], replicated
The draws below stay inside these ranges and needn't reach their ends.
Inputs may be any that keep to these rules, and one draw needn't show every extreme that they name: `doc_ids`: document numbers never fall along the stream; every document has 1 to 1280 tokens and one has exactly 1280. `span_of`: each span is held by exactly one index of ctx.
All inputs are finite; a program needn't handle non-finite values.
Results may differ from the reference program's by a relative error of at most 0.012.
The reference program's roundings to bfloat16 on the way (of `ordered`, `normed`, `weights` and `attended`) count: a program that leaves them out, or rounds other values in their place, can miss the bound.
Values may be sent and summed in bfloat16 or wider, within the bound.
No kernel may reach another device: no remote copies, remote signals or barrier semaphores. Data moves between devices by JAX's collectives and lax.ppermute only.
A program may use at most 192 MiB of HBM per device.

```python
import math
import jax
import jax.numpy as jnp
import numpy as np
from jax import lax

D = 8192
HEADS = 32
KVH = 8
HDIM = 128
BLOCK = 128
NDOC = 4
TOKENS = 4096
MOST = 1280
CARRY = 3
N_CTX = 8
N_TP = 4


def plant_directions(key):
    base = jax.random.fold_in(key, 7001)
    direction = (2 * jax.random.randint(jax.random.fold_in(base, 1), (D,), 0, 2) - 1).astype(jnp.float32)
    head_sign = (2 * jax.random.randint(jax.random.fold_in(base, 2), (KVH, HDIM), 0, 2) - 1).astype(jnp.float32)
    return (direction, head_sign)


def plant_strength():
    return 5.0


def weight_noise(key, columns, salt):
    noise_key = jax.random.fold_in(jax.random.fold_in(key, 7101), salt)
    noise = jnp.clip(jax.random.normal(noise_key, (D, columns), jnp.float32), -6.0, 6.0)
    return noise * D ** (-0.5)


def draw_w_query(key, part):
    direction, head_sign = plant_directions(key)
    pattern = jnp.repeat(head_sign, HEADS // KVH, 0).reshape(HEADS * HDIM)
    result = weight_noise(key, HEADS * HDIM, 11) + plant_strength() / D * direction[:, None] * pattern[None, :]
    return result.astype(jnp.bfloat16)


def draw_w_key(key, part):
    direction, head_sign = plant_directions(key)
    pattern = head_sign.reshape(KVH * HDIM)
    result = weight_noise(key, KVH * HDIM, 23) + plant_strength() / D * direction[:, None] * pattern[None, :]
    return result.astype(jnp.bfloat16)


def draw_tokens(key, part):
    direction, head_sign = plant_directions(key)
    run_count = 8
    run_length = 4
    starts = jax.random.randint(jax.random.fold_in(key, 7201), (run_count,), 0, TOKENS - run_length + 1)
    levels = jax.random.uniform(jax.random.fold_in(key, 7202), (run_count,), jnp.float32, 0.7, 0.98)
    row_iota = jnp.arange(TOKENS, dtype=jnp.int32)
    inside = (row_iota[:, None] >= starts[None, :]) & (row_iota[:, None] < starts[None, :] + run_length)
    level = jnp.max(jnp.where(inside, levels[None, :], 0.0), 1)
    noise_key = jax.random.fold_in(key, 7203)
    noise = jnp.clip(jax.random.normal(noise_key, (TOKENS, D), jnp.float32), -6.0, 6.0)
    rows = level[:, None] * direction[None, :] + jnp.sqrt(1.0 - level * level)[:, None] * noise
    return jnp.clip(rows, -6.0, 6.0).astype(jnp.bfloat16)


def block_levels(own_key, dims, shards, least, largest):
    level, own = 1.0, jax.random.fold_in(own_key, 6)
    for dim, parts in shards:
        draws = jnp.exp(jax.random.uniform(jax.random.fold_in(own, dim), (parts,), jnp.float32, least / len(shards), largest / len(shards)))
        level = level * jnp.repeat(draws, dims[dim] // parts).reshape([-1 if axis == dim else 1 for axis in range(len(dims))])
    return level


def profile(count, total, bound, lean):
    weights = [(1 << 20) // math.isqrt(rank ** lean) + 1 for rank in range(2, count + 1)]
    surplus, given = total - bound - (count - 1), [1] * (count - 1)
    while surplus > 0:
        movable = [i for i in range(count - 1) if given[i] < bound]
        whole, budget = sum([weights[i] for i in movable]), surplus
        for i in movable:
            more = min(bound - given[i], max(1, budget * weights[i] // whole), surplus)
            given[i] = given[i] + more
            surplus = surplus - more
    return np.array([bound] + given)


def uneven(key, number_of, total, limit, lean):
    if number_of == 2:
        one = jax.random.randint(key, (), max(1, total - limit), min(limit, total - 1) + 1)
        return jnp.stack([one, total - one])
    lengths = jnp.asarray(profile(number_of, total, limit, lean), jnp.int32)
    pairs = (number_of - 1) // 2
    giver, sink = lengths[1:1 + 2 * pairs:2], lengths[2:2 + 2 * pairs:2]
    room = jnp.minimum(giver - 1, limit - sink)
    moved = jax.random.randint(jax.random.fold_in(key, 1), (pairs,), 0, 1 << 20) % (room + 1)
    lengths = lengths.at[1:1 + 2 * pairs:2].set(giver - moved).at[2:2 + 2 * pairs:2].set(sink + moved)
    return lengths[jax.random.permutation(jax.random.fold_in(key, 2), number_of)]


def normal_values(rng, shape, scale, reach, shards=(), kind=jnp.bfloat16):
    level = block_levels(rng, shape, shards, -0.22, 0.18) if shards else 1.0
    values = jax.random.normal(rng, shape, jnp.float32) * scale * level
    return jnp.minimum(jnp.maximum(values, -reach), reach).astype(kind)


def setup_inputs(seed: int = 0) -> dict:
    arg_keys = jax.random.split(jax.random.key(seed), 14)
    tokens = draw_tokens(jax.random.fold_in(arg_keys[13], 71), 0)
    norm_gain = jnp.clip(1.0 + 0.18 * jax.random.normal(arg_keys[1], (D,), jnp.float32), 0.1, 1.9)
    w_query = draw_w_query(jax.random.fold_in(arg_keys[13], 71), 0)
    query_scale = jnp.clip(jnp.exp(math.log(2.0) - 1.3862944 * jax.random.uniform(arg_keys[3], (D // BLOCK, HEADS * HDIM // BLOCK), jnp.float32) ** block_levels(arg_keys[3], (D // BLOCK, HEADS * HDIM // BLOCK), ((1, 4),), -0.2, 0.2)), 0.5, 2.0)
    w_key = draw_w_key(jax.random.fold_in(arg_keys[13], 71), 0)
    key_scale = jnp.clip(jnp.exp(math.log(2.0) - 1.3862944 * jax.random.uniform(arg_keys[5], (D // BLOCK, KVH * HDIM // BLOCK), jnp.float32) ** block_levels(arg_keys[5], (D // BLOCK, KVH * HDIM // BLOCK), ((1, 4),), -0.2, 0.2)), 0.5, 2.0)
    w_value = normal_values(arg_keys[6], (D, KVH * HDIM), D ** -0.5, 0.0625, ((1, 4),))
    value_scale = jnp.clip(jnp.exp(math.log(2.0) - 1.3862944 * jax.random.uniform(arg_keys[7], (D // BLOCK, KVH * HDIM // BLOCK), jnp.float32) ** block_levels(arg_keys[7], (D // BLOCK, KVH * HDIM // BLOCK), ((1, 4),), -0.2, 0.2)), 0.5, 2.0)
    w_out = normal_values(arg_keys[8], (HEADS * HDIM, D), (HEADS * HDIM) ** -0.5, 0.09375, ((0, 4),))
    out_scale = jnp.clip(jnp.exp(math.log(2.0) - 1.3862944 * jax.random.uniform(arg_keys[9], (HEADS * HDIM // BLOCK, D // BLOCK), jnp.float32) ** block_levels(arg_keys[9], (HEADS * HDIM // BLOCK, D // BLOCK), ((0, 4),), -0.2, 0.2)), 0.5, 2.0)
    score_vec = normal_values(arg_keys[10], (D,), D ** -0.5, 0.0625)
    doc_ids = jnp.searchsorted(jnp.cumsum(uneven(arg_keys[11], NDOC, TOKENS, MOST, 2)), jnp.arange(TOKENS), side="right").astype(jnp.int32)
    span_of = jax.random.permutation(arg_keys[12], N_CTX).astype(jnp.int32)
    return {"tokens": tokens, "norm_gain": norm_gain, "w_query": w_query, "query_scale": query_scale, "w_key": w_key, "key_scale": key_scale, "w_value": w_value, "value_scale": value_scale, "w_out": w_out, "out_scale": out_scale, "score_vec": score_vec, "doc_ids": doc_ids, "span_of": span_of}


def rms_norm(values_in, gain):
    widened = values_in.astype(jnp.float32)
    factor = lax.rsqrt(lax.optimization_barrier(jnp.mean(widened * widened, -1, keepdims=True)) + 1e-05)
    return (widened * factor * gain).astype(jnp.bfloat16)

def dequant(stored, scales):
    expanded = jnp.repeat(jnp.repeat(scales, BLOCK, 0), BLOCK, 1)
    return (stored.astype(jnp.float32) * expanded).astype(jnp.bfloat16)

def rotate(heads_in, positions):
    half_dim = heads_in.shape[-1] // 2
    frequency = 500000.0 ** (-2.0 * jnp.arange(half_dim).astype(jnp.float32) / heads_in.shape[-1])
    angles = positions.astype(jnp.float32)[:, None] * frequency[None, :]
    cosine = jnp.cos(angles)[:, None, :]
    sine = jnp.sin(angles)[:, None, :]
    lower_half = heads_in[..., :half_dim]
    upper_half = heads_in[..., half_dim:]
    return jnp.concatenate([lower_half * cosine - upper_half * sine, upper_half * cosine + lower_half * sine], -1)

def reference(tokens, norm_gain, w_query, query_scale, w_key, key_scale, w_value, value_scale, w_out, out_scale, score_vec, doc_ids, span_of):
    span_len = TOKENS // N_CTX
    slot_iota = jnp.arange(N_CTX, dtype=jnp.int32)
    inverse = lax.optimization_barrier(jnp.sum(jnp.where(span_of[None, :] == slot_iota[:, None], slot_iota[None, :], 0), 1)).astype(jnp.int32)
    ordered = tokens.reshape(N_CTX, span_len, D)[inverse].reshape(TOKENS, D)
    doc_iota = jnp.arange(NDOC, dtype=jnp.int32)
    counts = lax.optimization_barrier(jnp.sum((doc_ids[:, None] == doc_iota[None, :]).astype(jnp.int32), 0))
    starts = jnp.cumsum(counts) - counts
    positions = jnp.arange(TOKENS, dtype=jnp.int32)
    relative = positions - starts[doc_ids]
    normed = rms_norm(ordered, norm_gain)
    queries = jnp.dot(normed, dequant(w_query, query_scale), preferred_element_type=jnp.float32)
    keys = jnp.dot(normed, dequant(w_key, key_scale), preferred_element_type=jnp.float32)
    values_all = jnp.dot(normed, dequant(w_value, value_scale), preferred_element_type=jnp.float32)
    queries = rotate(queries.reshape(TOKENS, HEADS, HDIM), relative).astype(jnp.bfloat16)
    keys = rotate(keys.reshape(TOKENS, KVH, HDIM), relative).astype(jnp.bfloat16)
    values_all = values_all.reshape(TOKENS, KVH, HDIM).astype(jnp.bfloat16)
    group = HEADS // KVH
    margin = CARRY * span_len
    window = margin + span_len
    key_pad = jnp.concatenate([jnp.zeros((margin, KVH, HDIM), jnp.bfloat16), keys], 0)
    value_pad = jnp.concatenate([jnp.zeros((margin, KVH, HDIM), jnp.bfloat16), values_all], 0)
    doc_pad = jnp.concatenate([jnp.full((margin,), -1, jnp.int32), doc_ids], 0)

    def one_span(span_index):
        first = (span_index * span_len).astype(jnp.int32)
        query_block = lax.dynamic_slice_in_dim(queries, first, span_len, 0).reshape(span_len, KVH, group, HDIM).astype(jnp.float32)
        key_block = lax.dynamic_slice_in_dim(key_pad, first, window, 0).astype(jnp.float32)
        value_block = lax.dynamic_slice_in_dim(value_pad, first, window, 0).astype(jnp.float32)
        key_doc = lax.dynamic_slice_in_dim(doc_pad, first, window, 0)
        query_doc = lax.dynamic_slice_in_dim(doc_ids, first, span_len, 0)
        query_pos = first + jnp.arange(span_len, dtype=jnp.int32)
        key_pos = first - margin + jnp.arange(window, dtype=jnp.int32)
        visible = (query_doc[:, None] == key_doc[None, :]) & (key_pos[None, :] <= query_pos[:, None])
        scores = jnp.einsum('qkgd,nkd->kgqn', query_block, key_block) * HDIM ** (-0.5)
        scores = jnp.where(visible[None, None], scores, -1e+30)
        peak = lax.optimization_barrier(jnp.max(scores, -1, keepdims=True))
        weights = jnp.where(visible[None, None], jnp.exp(scores - peak), 0.0)
        total = lax.optimization_barrier(jnp.sum(weights, -1))
        rounded = lax.optimization_barrier(weights.astype(jnp.bfloat16)).astype(jnp.float32)
        summed = jnp.einsum('kgqn,nkd->kgqd', rounded, value_block)
        result = summed / total[..., None]
        return result.transpose(2, 0, 1, 3).reshape(span_len, HEADS * HDIM).astype(jnp.bfloat16)
    attended = lax.map(one_span, jnp.arange(N_CTX, dtype=jnp.int32)).reshape(TOKENS, HEADS * HDIM)
    w_back = dequant(w_out, out_scale)
    per_group = HEADS * HDIM // N_TP
    mixed = jnp.zeros((TOKENS, D), jnp.float32)
    for group_index in range(N_TP):
        lower = group_index * per_group
        term = jnp.dot(attended[:, lower:lower + per_group], w_back[lower:lower + per_group], preferred_element_type=jnp.float32)
        mixed = mixed + lax.optimization_barrier(term.astype(jnp.bfloat16)).astype(jnp.float32)
    out_rows = (ordered.astype(jnp.float32) + mixed).astype(jnp.bfloat16)
    row_score = jnp.dot(out_rows, score_vec, preferred_element_type=jnp.float32)
    totals = jax.ops.segment_sum(row_score, doc_ids, num_segments=NDOC)
    doc_score = totals / counts.astype(jnp.float32)
    hidden = out_rows.reshape(N_CTX, span_len, D)[span_of].reshape(TOKENS, D)
    return (hidden, doc_score)
```

```python
import functools

import jax
import jax.numpy as jnp
from jax import lax
from jax.experimental import pallas as pl
from jax.experimental.pallas import tpu as pltpu
from jax.sharding import PartitionSpec as P

HDIM = 128
BLOCK = 128
NDOC = 4
F32 = jnp.float32
BF16 = jnp.bfloat16
ANY = pl.ANY
HBM = pltpu.HBM
VMEM = pltpu.VMEM
SMEM = pltpu.SMEM
MIB = 1 << 20


def params(mib):
    return pltpu.CompilerParams(vmem_limit_bytes=mib * MIB)


def cost(flops, moved):
    return pl.CostEstimate(flops=int(flops), bytes_accessed=int(moved), transcendentals=0)


def turn(values, cosine, sine):
    pieces = []
    for head in range(values.shape[1] // HDIM):
        one = values[:, head * HDIM : (head + 1) * HDIM]
        pieces.append(one * cosine + pltpu.roll(one, HDIM // 2, 1) * sine)
    return jnp.concatenate(pieces, 1)


def resident(value):
    return pltpu.with_memory_space_constraint(value, VMEM)


def outside(value):
    return pltpu.with_memory_space_constraint(value, HBM)


def normalize(parts, gain, normed):
    rows, half = parts[0].shape
    step, wide = 16, 1024
    for block in range(len(parts) // 2):
        pair = parts[2 * block : 2 * block + 2]

        @pl.loop(0, rows // step)
        def _(i):
            here = pl.ds(pl.multiple_of(i * step, step), step)
            there = pl.ds(pl.multiple_of(block * rows + i * step, step), step)
            square = jnp.zeros((step, wide), F32)
            for part in pair:
                for c in range(half // wide):
                    chunk = part[here, c * wide : (c + 1) * wide].astype(F32)
                    square = square + chunk * chunk
            factor = lax.rsqrt(jnp.sum(square, -1, keepdims=True) / (2 * half) + 1e-05)
            for side, part in enumerate(pair):
                for c in range(half // wide):
                    columns = slice(c * wide, (c + 1) * wide)
                    at = slice(side * half + c * wide, side * half + (c + 1) * wide)
                    chunk = part[here, columns].astype(F32)
                    normed[there, at] = (chunk * factor * gain[:, at]).astype(BF16)


def keys_and_values(normed, weight, cosine, sine, pair):
    key_cols = pair.shape[1] // 2
    product = jnp.dot(normed[...], weight[:, :key_cols], preferred_element_type=F32)
    pair[:, :key_cols] = turn(product, cosine[...], sine[...]).astype(BF16)
    product = jnp.dot(
        normed[...], weight[:, key_cols : 2 * key_cols], preferred_element_type=F32
    )
    pair[:, key_cols:] = product.astype(BF16)


def queries_of(normed, weight, skip, cosine, sine, query):
    tile = 2 * HDIM
    for start in range(0, query.shape[1], tile):
        product = jnp.dot(
            normed[...], weight[:, skip + start : skip + start + tile], preferred_element_type=F32
        )
        query[:, start : start + tile] = turn(product, cosine[...], sine[...]).astype(BF16)


def joint_body(count, *refs):
    stored, scales = refs[:count], refs[count : 2 * count]
    weight = refs[2 * count]
    slots, sems = refs[2 * count + 1 : 3 * count + 1], refs[3 * count + 1]
    depth = slots[0].shape[1]
    steps = weight.shape[0] // depth

    def fetch(i, slot):
        here = pl.ds(pl.multiple_of(i * depth, depth), depth)
        return [
            pltpu.make_async_copy(stored[n].at[here], slots[n].at[slot], sems.at[n, slot])
            for n in range(count)
        ]

    for copy in fetch(0, 0):
        copy.start()

    @pl.loop(0, steps)
    def _(i):
        slot = lax.rem(i, 2)

        @pl.when(i + 1 < steps)
        def _():
            for copy in fetch(i + 1, 1 - slot):
                copy.start()

        for copy in fetch(i, slot):
            copy.wait()
        for r in range(depth // BLOCK):
            out_rows = pl.ds(pl.multiple_of(i * depth + r * BLOCK, BLOCK), BLOCK)
            column = 0
            for n in range(count):
                for j in range(slots[n].shape[2] // BLOCK):
                    tile = slots[n][
                        slot, r * BLOCK : (r + 1) * BLOCK, j * BLOCK : (j + 1) * BLOCK
                    ].astype(F32)
                    factor = scales[n][i * (depth // BLOCK) + r, j]
                    weight[out_rows, column + j * BLOCK : column + (j + 1) * BLOCK] = (
                        tile * factor
                    ).astype(BF16)
                column += slots[n].shape[2]


def dequant_joint(stored, scales):
    width, depth = stored[0].shape[0], 512
    widths = [one.shape[1] for one in stored]
    return pl.pallas_call(
        functools.partial(joint_body, len(stored)),
        in_specs=[pl.BlockSpec(memory_space=HBM) for _ in widths]
        + [pl.BlockSpec(memory_space=SMEM) for _ in widths],
        out_specs=pl.BlockSpec(memory_space=VMEM),
        out_shape=VMEM((width, sum(widths)), BF16),
        scratch_shapes=[VMEM((2, depth, one), BF16) for one in widths]
        + [pltpu.SemaphoreType.DMA((len(widths), 2))],
        compiler_params=params(16),
        cost_estimate=cost(600 * width * sum(widths), 2 * width * sum(widths)),
    )(*[outside(one) for one in stored], *scales)


def keys_body(blocks, *refs):
    parts = refs[: 2 * blocks]
    gain, weight, cosine, sine, normed, pair = refs[2 * blocks :]
    normalize(parts, gain, normed)
    keys_and_values(normed, weight, cosine, sine, pair)


def project_keys(parts, rows, gain, weight, key_cols, cosine, sine):
    blocks = len(parts) // 2
    width = weight.shape[0]
    half, total = width // 2, rows * blocks
    inside = pl.BlockSpec(memory_space=VMEM)
    return pl.pallas_call(
        functools.partial(keys_body, blocks),
        grid=(1,),
        in_specs=[pl.BlockSpec((rows, half), lambda k, at=at: (0, at)) for _, at in parts]
        + [pl.BlockSpec((1, width), lambda k: (0, 0)), inside, inside, inside],
        out_specs=[pl.BlockSpec((total, width), lambda k: (0, 0)), inside],
        out_shape=[
            jax.ShapeDtypeStruct((total, width), BF16),
            jax.ShapeDtypeStruct((total, 2 * key_cols), BF16),
        ],
        compiler_params=params(16),
        cost_estimate=cost(8 * total * width * key_cols, 6 * total * width),
    )(*[one for one, _ in parts], gain, resident(weight), cosine, sine)


def queries_body(skip, normed, weight, cosine, sine, query):
    queries_of(normed, weight, skip, cosine, sine, query)


def project_queries(normed, weight, skip, cosine, sine):
    total, width = normed.shape
    columns = weight.shape[1] - skip
    inside = pl.BlockSpec(memory_space=VMEM)
    return pl.pallas_call(
        functools.partial(queries_body, skip),
        in_specs=[inside] * 4,
        out_specs=inside,
        out_shape=jax.ShapeDtypeStruct((total, columns), BF16),
        compiler_params=params(16),
        cost_estimate=cost(4 * total * width * columns, 4 * total * width),
    )(normed, resident(weight), cosine, sine)


def back_body(stored, scales, out, slots, sems):
    depth, width = slots.shape[1:]
    steps = stored.shape[0] // depth

    def fetch(i, slot):
        here = pl.ds(pl.multiple_of(i * depth, depth), depth)
        return pltpu.make_async_copy(stored.at[here], slots.at[slot], sems.at[slot])

    fetch(0, 0).start()

    @pl.loop(0, steps)
    def _(i):
        slot = lax.rem(i, 2)

        @pl.when(i + 1 < steps)
        def _():
            fetch(i + 1, 1 - slot).start()

        fetch(i, slot).wait()
        here = pl.ds(pl.multiple_of(i * depth, depth), depth)
        for j in range(width // BLOCK):
            there = slice(j * BLOCK, (j + 1) * BLOCK)
            factor = scales[i * depth // BLOCK, j]
            out[here, there] = (slots[slot, :, there].astype(F32) * factor).astype(BF16)


def dequant_back(stored, scales):
    rows, width = stored.shape
    depth = BLOCK
    return pl.pallas_call(
        back_body,
        in_specs=[pl.BlockSpec(memory_space=HBM), pl.BlockSpec(memory_space=SMEM)],
        out_specs=pl.BlockSpec(memory_space=VMEM),
        out_shape=VMEM((rows, width), BF16),
        scratch_shapes=[VMEM((2, depth, width), BF16), pltpu.SemaphoreType.DMA((2,))],
        compiler_params=params(8),
        cost_estimate=cost(8 * rows * width, 2 * rows * width),
    )(outside(stored), scales)


def toward_body(weight, vector, toward):
    rows, width = weight.shape
    step = 32

    @pl.loop(0, rows // step)
    def _(i):
        here = pl.ds(pl.multiple_of(i * step, step), step)
        run = jnp.zeros((step, BLOCK), F32)
        for j in range(width // BLOCK):
            there = slice(j * BLOCK, (j + 1) * BLOCK)
            run = run + weight[here, there].astype(F32) * vector[:, there]
        toward[here, :] = jnp.broadcast_to(jnp.sum(run, 1, keepdims=True), (step, BLOCK))


def toward_score(weight, vector):
    rows, width = weight.shape
    inside = pl.BlockSpec(memory_space=VMEM)
    return pl.pallas_call(
        toward_body,
        in_specs=[inside] * 2,
        out_specs=inside,
        out_shape=jax.ShapeDtypeStruct((rows, BLOCK), F32),
        compiler_params=params(8),
        cost_estimate=cost(8 * rows * width, 2 * rows * width),
    )(resident(weight), vector)


def halves_body(one, two, low, high):
    low[...] = one[...]
    high[...] = two[...]


def halves(one, two):
    rows, width = one.shape
    steps = 4
    tile = width // 2 // steps
    first = pl.BlockSpec((rows, tile), lambda j: (0, j))
    second = pl.BlockSpec((rows, tile), lambda j: (0, steps + j))
    return pl.pallas_call(
        halves_body,
        grid=(steps,),
        in_specs=[first, second],
        out_specs=[first, first],
        out_shape=[jax.ShapeDtypeStruct((rows, width // 2), BF16)] * 2,
        compiler_params=params(8),
        cost_estimate=cost(0, 4 * rows * width),
    )(one, two)


def attend_body(sizes, *refs):
    units, rows, kv_heads, group, chunk, kinds = sizes
    meta = refs[0]
    many = len(kinds)
    queries = refs[1 : 1 + many]
    held = refs[1 + many : 1 + many + many * units]
    out, pool, asked, kv_sem, q_sem = refs[1 + many + many * units :]
    length = sum(len(flips) for flips in kinds) * rows
    key_cols = kv_heads * HDIM
    mine = meta[0]
    starts = [meta[1 + d] for d in range(NDOC)]
    member = meta[1 + NDOC]
    span_at = 2 + NDOC

    def doc_start(position):
        found = jnp.int32(0)
        for one in starts:
            found = jnp.where(one <= position, one, found)
        return found

    first_span = doc_start(mine * length) // length
    q_copies = [
        pltpu.make_async_copy(
            queries[i],
            asked.at[pl.ds(flips[0] * rows, len(flips) * rows)],
            q_sem.at[i],
        )
        for i, flips in enumerate(kinds)
    ]
    for copy in q_copies:
        copy.start()

    def copies(unit, go):
        span = meta[span_at + unit]

        @pl.when((span >= first_span) & (span <= mine))
        def _():
            count = 0
            for kind, flips in enumerate(kinds):
                source = held[kind * units + unit]
                for piece, flip in enumerate(flips):
                    place = pl.multiple_of(
                        span * length + (member ^ flip) * rows, BLOCK
                    )
                    copy = pltpu.make_async_copy(
                        source.at[pl.ds(piece * rows, rows)],
                        pool.at[pl.ds(place, rows)],
                        kv_sem.at[unit, count],
                    )
                    count += 1
                    if go:
                        copy.start()
                    else:
                        copy.wait()

    for unit in range(units):
        copies(unit, True)
    for copy in q_copies:
        copy.wait()
    for unit in range(units):
        copies(unit, False)

    factor = HDIM ** (-0.5) * 1.4426950408889634

    @pl.loop(0, length // BLOCK)
    def _(index):
        at = pl.multiple_of(index * BLOCK, BLOCK)
        flip = at // rows
        position = mine * length + (member ^ flip) * rows + at % rows
        low = doc_start(position) // chunk
        high = (position + BLOCK - 1) // chunk
        row_pos = position + lax.broadcasted_iota(jnp.int32, (BLOCK, chunk), 0)
        row_start = doc_start(row_pos)
        lane = lax.broadcasted_iota(jnp.int32, (BLOCK, chunk), 1)
        for head in range(kv_heads):
            query = jnp.concatenate(
                [
                    asked[
                        pl.ds(at, BLOCK),
                        (head * group + g) * HDIM : (head * group + g + 1) * HDIM,
                    ]
                    for g in range(group)
                ],
                0,
            )

            def one_chunk(c, state):
                peak, total, acc = state
                here = pl.ds(pl.multiple_of(c * chunk, chunk), chunk)
                key = pool[here, head * HDIM : (head + 1) * HDIM]
                value = pool[here, key_cols + head * HDIM : key_cols + (head + 1) * HDIM]
                scores = lax.dot_general(
                    query, key, (((1,), (1,)), ((), ())), preferred_element_type=F32
                )
                key_pos = lane + c * chunk
                seen = (key_pos <= row_pos) & (key_pos >= row_start)
                scores = jnp.where(
                    seen[None], scores.reshape(group, BLOCK, chunk) * factor, -1e30
                ).reshape(group * BLOCK, chunk)
                higher = jnp.maximum(peak, jnp.max(scores, -1, keepdims=True))
                weights = jnp.exp2(scores - higher)
                fading = jnp.exp2(peak - higher)
                total = total * fading + jnp.sum(weights, -1, keepdims=True)
                acc = acc * fading + jnp.dot(
                    weights.astype(BF16), value, preferred_element_type=F32
                )
                return higher, total, acc

            state = (
                jnp.full((group * BLOCK, 1), -1e30, F32),
                jnp.zeros((group * BLOCK, 1), F32),
                jnp.zeros((group * BLOCK, HDIM), F32),
            )
            peak, total, acc = lax.fori_loop(low, high + 1, one_chunk, state)
            result = (acc / total).astype(BF16)
            for g in range(group):
                out[
                    pl.ds(at, BLOCK), (head * group + g) * HDIM : (head * group + g + 1) * HDIM
                ] = result[g * BLOCK : (g + 1) * BLOCK]


def attend(meta, queries, held, units, rows, kv_heads, group, kinds):
    blocks = sum(len(flips) for flips in kinds)
    length = blocks * rows
    columns = kv_heads * group * HDIM
    chunk = 2 * BLOCK
    sizes = (units, rows, kv_heads, group, chunk, kinds)
    return pl.pallas_call(
        functools.partial(attend_body, sizes),
        in_specs=[pl.BlockSpec(memory_space=SMEM)]
        + [pl.BlockSpec(memory_space=ANY)] * (len(kinds) * (1 + units)),
        out_specs=pl.BlockSpec(memory_space=VMEM),
        out_shape=jax.ShapeDtypeStruct((length, columns), BF16),
        scratch_shapes=[
            VMEM((units * length, 2 * kv_heads * HDIM), BF16),
            VMEM((length, columns), BF16),
            pltpu.SemaphoreType.DMA((units, blocks)),
            pltpu.SemaphoreType.DMA((len(kinds),)),
        ],
        compiler_params=params(20),
        cost_estimate=cost(8 * length * columns * 1024, 8 * MIB),
    )(meta, *queries, *held)


def term_of(rows_of, weight, start, width):
    return jnp.dot(
        rows_of, weight[:, start : start + width], preferred_element_type=F32
    ).astype(BF16)


def outward_body(starts, attended, weight, xo, yo):
    rows = attended.shape[0] // 4
    tile = 512
    for start in range(0, xo.shape[1], tile):
        here = slice(start, start + tile)
        for block, place in ((1, 0), (3, rows)):
            xo[place : place + rows, here] = term_of(
                attended[block * rows : (block + 1) * rows, :], weight, starts[0] + start, tile
            )
        for block, place in ((2, 0), (3, rows)):
            yo[place : place + rows, here] = term_of(
                attended[block * rows : (block + 1) * rows, :], weight, starts[1] + start, tile
            )


def outward(attended, weight, start, span):
    depth, width = weight.shape
    rows = attended.shape[0] // 4
    inside = pl.BlockSpec(memory_space=VMEM)
    return pl.pallas_call(
        functools.partial(outward_body, (start, width // 2 + start)),
        in_specs=[inside] * 2,
        out_specs=[inside] * 2,
        out_shape=[jax.ShapeDtypeStruct((2 * rows, span), BF16)] * 2,
        compiler_params=params(12),
        cost_estimate=cost(16 * rows * depth * span, 8 * rows * span),
    )(attended, resident(weight))


def kept_body(attended, weight, inner, term):
    rows = attended.shape[0] // 4
    width = weight.shape[1]
    tile = 512
    for start in range(0, width, tile):
        here = slice(start, start + tile)
        block = 2 if start < width // 2 else 1
        inner[:, here] = term_of(
            attended[block * rows : (block + 1) * rows, :], weight, start, tile
        )
        term[:, here] = term_of(attended[:rows, :], weight, start, tile)


def kept_terms(attended, weight):
    depth, width = weight.shape
    rows = attended.shape[0] // 4
    inside = pl.BlockSpec(memory_space=VMEM)
    return pl.pallas_call(
        kept_body,
        in_specs=[inside] * 2,
        out_specs=[inside] * 2,
        out_shape=[jax.ShapeDtypeStruct((rows, width), BF16)] * 2,
        compiler_params=params(12),
        cost_estimate=cost(8 * rows * depth * width, 4 * rows * width),
    )(attended, resident(weight))


def block_body(block, blocks, attended, weight, out):
    rows = attended.shape[0] // blocks
    for start in range(0, weight.shape[1], 512):
        out[:, start : start + 512] = term_of(
            attended[block * rows : (block + 1) * rows, :], weight, start, 512
        )


def block_term(attended, weight, block, blocks):
    depth, width = weight.shape
    rows = attended.shape[0] // blocks
    inside = pl.BlockSpec(memory_space=VMEM)
    return pl.pallas_call(
        functools.partial(block_body, block, blocks),
        in_specs=[inside] * 2,
        out_specs=inside,
        out_shape=jax.ShapeDtypeStruct((rows, width), BF16),
        compiler_params=params(12),
        cost_estimate=cost(2 * rows * depth * width, 2 * rows * width),
    )(attended, resident(weight))


def finish_body(token, term, near_x, near_y, far_y, far_x, *rest):
    out = rest[-1]

    def add(near, far):
        mixed = term[...].astype(F32) + near[...].astype(F32) + far[...].astype(F32)
        out[...] = (token[...].astype(F32) + mixed).astype(BF16)

    @pl.when(pl.program_id(0) == 0)
    def _():
        add(near_x, far_y)

    @pl.when(pl.program_id(0) == 1)
    def _():
        add(near_y, far_x)


def finish(token, term, near_x, near_y, far_y, far_x, before, part, parts):
    rows, width = token.shape
    span = width // 2 // parts
    tile = min(span, 1024)
    steps = span // tile
    half = width // 2 // tile

    def whole(h, j):
        return (0, h * half + part * steps + j)

    low = pl.BlockSpec((rows, tile), lambda h, j: (0, jnp.where(h == 0, j, steps - 1)))
    high = pl.BlockSpec((rows, tile), lambda h, j: (0, jnp.where(h == 0, 0, j)))
    specs = [pl.BlockSpec((rows, tile), whole)] * 2 + [low, high, low, high]
    operands = [token, term, near_x, near_y, far_y, far_x]
    aliases = {}
    if before is not None:
        specs.append(pl.BlockSpec(memory_space=ANY))
        operands.append(before)
        aliases = {6: 0}
    return pl.pallas_call(
        finish_body,
        grid=(2, steps),
        in_specs=specs,
        out_specs=pl.BlockSpec((rows, tile), whole),
        out_shape=jax.ShapeDtypeStruct((rows, width), BF16),
        input_output_aliases=aliases,
        compiler_params=params(40),
        cost_estimate=cost(rows * span, 20 * rows * span),
    )(*operands)


def on_device(
    tokens,
    norm_gain,
    w_query,
    query_scale,
    w_key,
    key_scale,
    w_value,
    value_scale,
    w_out,
    out_scale,
    score_vec,
    doc_ids,
    span_of,
):
    rows, width = tokens.shape
    half = width // 2
    n_ctx = lax.axis_size("ctx")
    n_tp = lax.axis_size("tp")
    length = n_tp * rows
    slot = lax.axis_index("ctx")
    member = lax.axis_index("tp")
    span_pos = span_of[slot]

    def flip_tp(value, flip):
        return lax.ppermute(value, "tp", [(i, i ^ flip) for i in range(n_tp)])

    query_cols, key_cols = w_query.shape[1], w_key.shape[1]
    kv_heads = key_cols // HDIM
    group = query_cols // key_cols
    gain = norm_gain[None, :]

    doc_iota = jnp.arange(NDOC, dtype=jnp.int32)
    counts = jnp.sum((doc_ids[None, :] == doc_iota[:, None]).astype(jnp.int32), 1)
    starts = jnp.sum(jnp.where(doc_iota[None, :] < doc_iota[:, None], counts[None, :], 0), 1)
    row_iota = jnp.arange(length, dtype=jnp.int32)
    position = span_pos * length + (member ^ (row_iota // rows)) * rows + row_iota % rows
    begun = starts[None, :] <= position[:, None]
    document = jnp.sum(begun.astype(jnp.int32), 1) - 1
    relative = position - jnp.max(jnp.where(begun, starts[None, :], 0), 1)
    frequency = 500000.0 ** (-2.0 * jnp.arange(HDIM // 2).astype(F32) / HDIM)
    angles = relative.astype(F32)[:, None] * frequency[None, :]
    cosine, sine = jnp.cos(angles), jnp.sin(angles)
    cosine = jnp.concatenate([cosine, cosine], 1)
    sine = jnp.concatenate([-sine, sine], 1)

    def exchange_along(value):
        return [value] + [
            lax.ppermute(value, "ctx", [(i, (i + 2 * step) % n_ctx) for i in range(n_ctx)])
            for step in range(1, n_ctx // 2)
        ]

    def exchange_across(held):
        return held + [
            lax.ppermute(one, "ctx", [(i, i ^ 1) for i in range(n_ctx)]) for one in held
        ]

    sources = [(slot - 2 * step) % n_ctx for step in range(n_ctx // 2)]
    sources += [((slot ^ 1) - 2 * step) % n_ctx for step in range(n_ctx // 2)]
    meta = jnp.concatenate(
        [
            span_pos[None],
            starts,
            member[None].astype(jnp.int32),
            jnp.take(span_of, jnp.stack(sources)),
        ]
    ).astype(jnp.int32)

    square = n_tp == 4
    if square:
        kinds = ((0,), (1, 2), (3,))
    else:
        kinds = ((0,),) + tuple((i, i + 1) for i in range(1, n_tp - 1, 2)) + ((n_tp - 1,),)
    tables = [
        tuple(
            one[flips[0] * rows : (flips[-1] + 1) * rows] for one in (cosine, sine)
        )
        for flips in kinds
    ]
    token_score = jnp.dot(tokens, score_vec, preferred_element_type=F32)
    vector = score_vec.astype(F32)[None, :]
    gain, tables, token_score, vector, meta, document, counts = lax.optimization_barrier(
        (gain, tables, token_score, vector, meta, document, counts)
    )
    near = {flip: flip_tp(tokens, flip) for flip in ((1, 2) if square else range(1, n_tp))}

    weight = dequant_joint((w_key, w_value, w_query), (key_scale, value_scale, query_scale))
    normed, own_pair = project_keys(
        [(tokens, 0), (tokens, 1)], rows, gain, weight, key_cols, *tables[0]
    )
    held = exchange_across(exchange_along(own_pair))
    own_query = project_queries(normed, weight, 2 * key_cols, *tables[0])

    if square:
        near[1], near[2], own_query = lax.optimization_barrier((near[1], near[2], own_query))
        low, high = halves(near[1], near[2])
        far_low, far_high = flip_tp(low, 2), flip_tp(high, 1)
    queries = [own_query]
    for flips, table in zip(kinds[1:], tables[1:]):
        if square and flips == (3,):
            far_low, far_high, queries = lax.optimization_barrier((far_low, far_high, queries))
            parts = [(far_low, 0), (far_high, 0)]
        else:
            parts = [(near[flip], side) for flip in flips for side in range(2)]
        normed, pair = project_keys(parts, rows, gain, weight, key_cols, *table)
        along = exchange_along(pair)
        query = project_queries(normed, weight, 2 * key_cols, *table)
        if flips == kinds[-1]:
            query, late_scale = lax.optimization_barrier((query, out_scale))
            back = dequant_back(w_out, late_scale)
            along, query, back = lax.optimization_barrier((along, query, back))
        held += exchange_across(along)
        queries.append(query)

    attended = attend(meta, queries, held, n_ctx, rows, kv_heads, group, kinds)

    def all_sum(value, axis, size, step):
        while step < size:
            value = value + lax.ppermute(value, axis, [(i, i ^ step) for i in range(size)])
            step *= 2
        return value

    def span_sums(attended, toward):
        row_score = jnp.sum(attended.astype(F32) * toward[:, 0][None, :], 1)
        row_score = row_score + jnp.concatenate([token_score, jnp.zeros((length - rows,), F32)])
        own = document[:, None] == doc_iota[None, :]
        partial = jnp.sum(jnp.where(own, row_score[:, None], 0.0), 0)
        return all_sum(partial, "ctx", n_ctx, 1)

    if not square:
        partial = span_sums(attended, toward_score(back, vector))
        mixed = block_term(attended, back, 0, n_tp).astype(F32)
        for flip in range(1, n_tp):
            mixed = mixed + flip_tp(block_term(attended, back, flip, n_tp), flip).astype(F32)
        totals = all_sum(partial, "tp", n_tp, 1)
        return ((tokens.astype(F32) + mixed).astype(BF16), totals / counts.astype(F32))

    parts = 2
    span = half // parts
    sent = []
    for part in range(parts):
        out_x, out_y = outward(attended, back, part * span, span)
        sent.append((flip_tp(out_x, 1), flip_tp(out_y, 2)))
        attended, out_x, out_y = lax.optimization_barrier((attended, out_x, out_y))
    inner, term = kept_terms(attended, back)
    partial = span_sums(attended, toward_score(back, vector))

    def onward(got, start):
        ours = inner[:, start : start + span].astype(F32)
        return (ours + got[rows:].astype(F32)).astype(BF16)

    hidden = None
    for part in range(parts):
        near_x, near_y = sent[part]
        near_x, near_y, inner, term, partial = lax.optimization_barrier(
            (near_x, near_y, inner, term, partial)
        )
        on_y, on_x = onward(near_x, part * span), onward(near_y, half + part * span)
        far_y, far_x = flip_tp(on_y, 2), flip_tp(on_x, 1)
        if part < 2:
            partial, on_y, on_x = lax.optimization_barrier((partial, on_y, on_x))
            partial = partial + flip_tp(partial, 1 + part)
        hidden = finish(tokens, term, near_x, near_y, far_y, far_x, hidden, part, parts)
    return (hidden, partial / counts.astype(F32))


def solution(mesh):
    return jax.shard_map(
        on_device,
        mesh=mesh,
        in_specs=(
            P(("ctx", "tp"), None),
            P(),
            P(None, "tp"),
            P(None, "tp"),
            P(None, "tp"),
            P(None, "tp"),
            P(None, "tp"),
            P(None, "tp"),
            P("tp", None),
            P("tp", None),
            P(),
            P(),
            P(),
        ),
        out_specs=(P(("ctx", "tp"), None), P()),
        check_vma=False,
    )
```

```python
import functools

import jax
import jax.numpy as jnp
from jax import lax
from jax.experimental import pallas as pl
from jax.experimental.pallas import tpu as pltpu
from jax.sharding import PartitionSpec as P

HDIM = 128
BLOCK = 128
NDOC = 4
F32 = jnp.float32
BF16 = jnp.bfloat16
ANY = pl.ANY
HBM = pltpu.HBM
VMEM = pltpu.VMEM
SMEM = pltpu.SMEM
MIB = 1 << 20


def params(mib):
    return pltpu.CompilerParams(vmem_limit_bytes=mib * MIB)


def cost(flops, moved):
    return pl.CostEstimate(flops=int(flops), bytes_accessed=int(moved), transcendentals=0)


def turn(values, cosine, sine):
    pieces = []
    for head in range(values.shape[1] // HDIM):
        one = values[:, head * HDIM : (head + 1) * HDIM]
        pieces.append(one * cosine + pltpu.roll(one, HDIM // 2, 1) * sine)
    return jnp.concatenate(pieces, 1)


def resident(value):
    return pltpu.with_memory_space_constraint(value, VMEM)


def outside(value):
    return pltpu.with_memory_space_constraint(value, HBM)


def normalize(parts, gain, normed):
    rows, half = parts[0].shape
    step, wide = 16, 1024
    for block in range(len(parts) // 2):
        pair = parts[2 * block : 2 * block + 2]

        @pl.loop(0, rows // step)
        def _(i):
            here = pl.ds(pl.multiple_of(i * step, step), step)
            there = pl.ds(pl.multiple_of(block * rows + i * step, step), step)
            square = jnp.zeros((step, wide), F32)
            for part in pair:
                for c in range(half // wide):
                    chunk = part[here, c * wide : (c + 1) * wide].astype(F32)
                    square = square + chunk * chunk
            factor = lax.rsqrt(jnp.sum(square, -1, keepdims=True) / (2 * half) + 1e-05)
            for side, part in enumerate(pair):
                for c in range(half // wide):
                    columns = slice(c * wide, (c + 1) * wide)
                    at = slice(side * half + c * wide, side * half + (c + 1) * wide)
                    chunk = part[here, columns].astype(F32)
                    normed[there, at] = (chunk * factor * gain[:, at]).astype(BF16)


def keys_and_values(normed, weight, cosine, sine, pair):
    key_cols = pair.shape[1] // 2
    product = jnp.dot(normed[...], weight[:, :key_cols], preferred_element_type=F32)
    pair[:, :key_cols] = turn(product, cosine[...], sine[...]).astype(BF16)
    product = jnp.dot(
        normed[...], weight[:, key_cols : 2 * key_cols], preferred_element_type=F32
    )
    pair[:, key_cols:] = product.astype(BF16)


def queries_of(normed, weight, skip, cosine, sine, query):
    tile = 2 * HDIM
    for start in range(0, query.shape[1], tile):
        product = jnp.dot(
            normed[...], weight[:, skip + start : skip + start + tile], preferred_element_type=F32
        )
        query[:, start : start + tile] = turn(product, cosine[...], sine[...]).astype(BF16)


def joint_body(count, *refs):
    stored, scales = refs[:count], refs[count : 2 * count]
    weight = refs[2 * count]
    slots, sems = refs[2 * count + 1 : 3 * count + 1], refs[3 * count + 1]
    depth = slots[0].shape[1]
    steps = weight.shape[0] // depth

    def fetch(i, slot):
        here = pl.ds(pl.multiple_of(i * depth, depth), depth)
        return [
            pltpu.make_async_copy(stored[n].at[here], slots[n].at[slot], sems.at[n, slot])
            for n in range(count)
        ]

    for copy in fetch(0, 0):
        copy.start()

    @pl.loop(0, steps)
    def _(i):
        slot = lax.rem(i, 2)

        @pl.when(i + 1 < steps)
        def _():
            for copy in fetch(i + 1, 1 - slot):
                copy.start()

        for copy in fetch(i, slot):
            copy.wait()
        for r in range(depth // BLOCK):
            out_rows = pl.ds(pl.multiple_of(i * depth + r * BLOCK, BLOCK), BLOCK)
            column = 0
            for n in range(count):
                for j in range(slots[n].shape[2] // BLOCK):
                    tile = slots[n][
                        slot, r * BLOCK : (r + 1) * BLOCK, j * BLOCK : (j + 1) * BLOCK
                    ].astype(F32)
                    factor = scales[n][i * (depth // BLOCK) + r, j]
                    weight[out_rows, column + j * BLOCK : column + (j + 1) * BLOCK] = (
                        tile * factor
                    ).astype(BF16)
                column += slots[n].shape[2]


def dequant_joint(stored, scales):
    width, depth = stored[0].shape[0], 512
    widths = [one.shape[1] for one in stored]
    return pl.pallas_call(
        functools.partial(joint_body, len(stored)),
        in_specs=[pl.BlockSpec(memory_space=HBM) for _ in widths]
        + [pl.BlockSpec(memory_space=SMEM) for _ in widths],
        out_specs=pl.BlockSpec(memory_space=VMEM),
        out_shape=VMEM((width, sum(widths)), BF16),
        scratch_shapes=[VMEM((2, depth, one), BF16) for one in widths]
        + [pltpu.SemaphoreType.DMA((len(widths), 2))],
        compiler_params=params(6),
        cost_estimate=cost(600 * width * sum(widths), 2 * width * sum(widths)),
    )(*[outside(one) for one in stored], *scales)


def keys_body(blocks, *refs):
    parts = refs[: 2 * blocks]
    gain, weight, cosine, sine, normed, pair = refs[2 * blocks :]
    normalize(parts, gain, normed)
    keys_and_values(normed, weight, cosine, sine, pair)


def project_keys(parts, rows, gain, weight, key_cols, cosine, sine):
    blocks = len(parts) // 2
    width = weight.shape[0]
    half, total = width // 2, rows * blocks
    inside = pl.BlockSpec(memory_space=VMEM)
    return pl.pallas_call(
        functools.partial(keys_body, blocks),
        grid=(1,),
        in_specs=[pl.BlockSpec((rows, half), lambda k, at=at: (0, at)) for _, at in parts]
        + [pl.BlockSpec((1, width), lambda k: (0, 0)), inside, inside, inside],
        out_specs=[pl.BlockSpec((total, width), lambda k: (0, 0)), inside],
        out_shape=[
            jax.ShapeDtypeStruct((total, width), BF16),
            jax.ShapeDtypeStruct((total, 2 * key_cols), BF16),
        ],
        compiler_params=params(6),
        cost_estimate=cost(8 * total * width * key_cols, 6 * total * width),
    )(*[one for one, _ in parts], gain, resident(weight), cosine, sine)


def queries_body(skip, normed, weight, cosine, sine, query):
    queries_of(normed, weight, skip, cosine, sine, query)


def project_queries(normed, weight, skip, cosine, sine):
    total, width = normed.shape
    columns = weight.shape[1] - skip
    inside = pl.BlockSpec(memory_space=VMEM)
    return pl.pallas_call(
        functools.partial(queries_body, skip),
        in_specs=[inside] * 4,
        out_specs=inside,
        out_shape=jax.ShapeDtypeStruct((total, columns), BF16),
        compiler_params=params(6),
        cost_estimate=cost(4 * total * width * columns, 4 * total * width),
    )(normed, resident(weight), cosine, sine)


def back_body(stored, scales, out, slots, sems):
    depth, width = slots.shape[1:]
    steps = stored.shape[0] // depth

    def fetch(i, slot):
        here = pl.ds(pl.multiple_of(i * depth, depth), depth)
        return pltpu.make_async_copy(stored.at[here], slots.at[slot], sems.at[slot])

    fetch(0, 0).start()

    @pl.loop(0, steps)
    def _(i):
        slot = lax.rem(i, 2)

        @pl.when(i + 1 < steps)
        def _():
            fetch(i + 1, 1 - slot).start()

        fetch(i, slot).wait()
        here = pl.ds(pl.multiple_of(i * depth, depth), depth)
        for j in range(width // BLOCK):
            there = slice(j * BLOCK, (j + 1) * BLOCK)
            factor = scales[i * depth // BLOCK, j]
            out[here, there] = (slots[slot, :, there].astype(F32) * factor).astype(BF16)


def dequant_back(stored, scales):
    rows, width = stored.shape
    depth = BLOCK
    return pl.pallas_call(
        back_body,
        in_specs=[pl.BlockSpec(memory_space=HBM), pl.BlockSpec(memory_space=SMEM)],
        out_specs=pl.BlockSpec(memory_space=VMEM),
        out_shape=VMEM((rows, width), BF16),
        scratch_shapes=[VMEM((2, depth, width), BF16), pltpu.SemaphoreType.DMA((2,))],
        compiler_params=params(5),
        cost_estimate=cost(8 * rows * width, 2 * rows * width),
    )(outside(stored), scales)


def toward_body(weight, vector, toward):
    rows, width = weight.shape
    step = 32

    @pl.loop(0, rows // step)
    def _(i):
        here = pl.ds(pl.multiple_of(i * step, step), step)
        run = jnp.zeros((step, BLOCK), F32)
        for j in range(width // BLOCK):
            there = slice(j * BLOCK, (j + 1) * BLOCK)
            run = run + weight[here, there].astype(F32) * vector[:, there]
        toward[here, :] = jnp.broadcast_to(jnp.sum(run, 1, keepdims=True), (step, BLOCK))


def toward_score(weight, vector):
    rows, width = weight.shape
    inside = pl.BlockSpec(memory_space=VMEM)
    return pl.pallas_call(
        toward_body,
        in_specs=[inside] * 2,
        out_specs=inside,
        out_shape=jax.ShapeDtypeStruct((rows, BLOCK), F32),
        compiler_params=params(5),
        cost_estimate=cost(8 * rows * width, 2 * rows * width),
    )(resident(weight), vector)


def halves_body(one, two, low, high):
    low[...] = one[...]
    high[...] = two[...]


def halves(one, two):
    rows, width = one.shape
    steps = 4
    tile = width // 2 // steps
    first = pl.BlockSpec((rows, tile), lambda j: (0, j))
    second = pl.BlockSpec((rows, tile), lambda j: (0, steps + j))
    return pl.pallas_call(
        halves_body,
        grid=(steps,),
        in_specs=[first, second],
        out_specs=[first, first],
        out_shape=[jax.ShapeDtypeStruct((rows, width // 2), BF16)] * 2,
        compiler_params=params(5),
        cost_estimate=cost(0, 4 * rows * width),
    )(one, two)


def attend_body(sizes, *refs):
    units, rows, kv_heads, group, chunk, kinds = sizes
    meta = refs[0]
    many = len(kinds)
    queries = refs[1 : 1 + many]
    held = refs[1 + many : 1 + many + many * units]
    out, pool, asked, kv_sem, q_sem = refs[1 + many + many * units :]
    length = sum(len(flips) for flips in kinds) * rows
    key_cols = kv_heads * HDIM
    mine = meta[0]
    starts = [meta[1 + d] for d in range(NDOC)]
    member = meta[1 + NDOC]
    span_at = 2 + NDOC

    def doc_start(position):
        found = jnp.int32(0)
        for one in starts:
            found = jnp.where(one <= position, one, found)
        return found

    first_span = doc_start(mine * length) // length
    q_copies = [
        pltpu.make_async_copy(
            queries[i],
            asked.at[pl.ds(flips[0] * rows, len(flips) * rows)],
            q_sem.at[i],
        )
        for i, flips in enumerate(kinds)
    ]
    for copy in q_copies:
        copy.start()

    def copies(unit, go):
        span = meta[span_at + unit]

        @pl.when((span >= first_span) & (span <= mine))
        def _():
            count = 0
            for kind, flips in enumerate(kinds):
                source = held[kind * units + unit]
                for piece, flip in enumerate(flips):
                    place = pl.multiple_of(
                        span * length + (member ^ flip) * rows, BLOCK
                    )
                    copy = pltpu.make_async_copy(
                        source.at[pl.ds(piece * rows, rows)],
                        pool.at[pl.ds(place, rows)],
                        kv_sem.at[unit, count],
                    )
                    count += 1
                    if go:
                        copy.start()
                    else:
                        copy.wait()

    for unit in range(units):
        copies(unit, True)
    for copy in q_copies:
        copy.wait()
    for unit in range(units):
        copies(unit, False)

    factor = HDIM ** (-0.5) * 1.4426950408889634

    @pl.loop(0, length // BLOCK)
    def _(index):
        at = pl.multiple_of(index * BLOCK, BLOCK)
        flip = at // rows
        position = mine * length + (member ^ flip) * rows + at % rows
        low = doc_start(position) // chunk
        high = (position + BLOCK - 1) // chunk
        row_pos = position + lax.broadcasted_iota(jnp.int32, (BLOCK, chunk), 0)
        row_start = doc_start(row_pos)
        lane = lax.broadcasted_iota(jnp.int32, (BLOCK, chunk), 1)
        for head in range(kv_heads):
            query = jnp.concatenate(
                [
                    asked[
                        pl.ds(at, BLOCK),
                        (head * group + g) * HDIM : (head * group + g + 1) * HDIM,
                    ]
                    for g in range(group)
                ],
                0,
            )

            def one_chunk(c, state):
                peak, total, acc = state
                here = pl.ds(pl.multiple_of(c * chunk, chunk), chunk)
                key = pool[here, head * HDIM : (head + 1) * HDIM]
                value = pool[here, key_cols + head * HDIM : key_cols + (head + 1) * HDIM]
                scores = lax.dot_general(
                    query, key, (((1,), (1,)), ((), ())), preferred_element_type=F32
                )
                key_pos = lane + c * chunk
                seen = (key_pos <= row_pos) & (key_pos >= row_start)
                scores = jnp.where(
                    seen[None], scores.reshape(group, BLOCK, chunk) * factor, -1e30
                ).reshape(group * BLOCK, chunk)
                higher = jnp.maximum(peak, jnp.max(scores, -1, keepdims=True))
                weights = jnp.exp2(scores - higher)
                fading = jnp.exp2(peak - higher)
                total = total * fading + jnp.sum(weights, -1, keepdims=True)
                acc = acc * fading + jnp.dot(
                    weights.astype(BF16), value, preferred_element_type=F32
                )
                return higher, total, acc

            state = (
                jnp.full((group * BLOCK, 1), -1e30, F32),
                jnp.zeros((group * BLOCK, 1), F32),
                jnp.zeros((group * BLOCK, HDIM), F32),
            )
            peak, total, acc = lax.fori_loop(low, high + 1, one_chunk, state)
            result = (acc / total).astype(BF16)
            for g in range(group):
                out[
                    pl.ds(at, BLOCK), (head * group + g) * HDIM : (head * group + g + 1) * HDIM
                ] = result[g * BLOCK : (g + 1) * BLOCK]


def attend(meta, queries, held, units, rows, kv_heads, group, kinds):
    blocks = sum(len(flips) for flips in kinds)
    length = blocks * rows
    columns = kv_heads * group * HDIM
    chunk = 2 * BLOCK
    sizes = (units, rows, kv_heads, group, chunk, kinds)
    return pl.pallas_call(
        functools.partial(attend_body, sizes),
        in_specs=[pl.BlockSpec(memory_space=SMEM)]
        + [pl.BlockSpec(memory_space=ANY)] * (len(kinds) * (1 + units)),
        out_specs=pl.BlockSpec(memory_space=VMEM),
        out_shape=jax.ShapeDtypeStruct((length, columns), BF16),
        scratch_shapes=[
            VMEM((units * length, 2 * kv_heads * HDIM), BF16),
            VMEM((length, columns), BF16),
            pltpu.SemaphoreType.DMA((units, blocks)),
            pltpu.SemaphoreType.DMA((len(kinds),)),
        ],
        compiler_params=params(
            3 + 4 * (units * length * kv_heads * HDIM + length * columns) // MIB
        ),
        cost_estimate=cost(8 * length * columns * 1024, 8 * MIB),
    )(meta, *queries, *held)


def term_of(rows_of, weight, start, width):
    return jnp.dot(
        rows_of, weight[:, start : start + width], preferred_element_type=F32
    ).astype(BF16)


def outward_body(starts, attended, weight, xo, yo):
    rows = attended.shape[0] // 4
    tile = 512
    for start in range(0, xo.shape[1], tile):
        here = slice(start, start + tile)
        for block, place in ((1, 0), (3, rows)):
            xo[place : place + rows, here] = term_of(
                attended[block * rows : (block + 1) * rows, :], weight, starts[0] + start, tile
            )
        for block, place in ((2, 0), (3, rows)):
            yo[place : place + rows, here] = term_of(
                attended[block * rows : (block + 1) * rows, :], weight, starts[1] + start, tile
            )


def outward(attended, weight, start, span):
    depth, width = weight.shape
    rows = attended.shape[0] // 4
    inside = pl.BlockSpec(memory_space=VMEM)
    return pl.pallas_call(
        functools.partial(outward_body, (start, width // 2 + start)),
        in_specs=[inside] * 2,
        out_specs=[inside] * 2,
        out_shape=[jax.ShapeDtypeStruct((2 * rows, span), BF16)] * 2,
        compiler_params=params(12),
        cost_estimate=cost(16 * rows * depth * span, 8 * rows * span),
    )(attended, resident(weight))


def kept_body(attended, weight, inner, term):
    rows = attended.shape[0] // 4
    width = weight.shape[1]
    tile = 512
    for start in range(0, width, tile):
        here = slice(start, start + tile)
        block = 2 if start < width // 2 else 1
        inner[:, here] = term_of(
            attended[block * rows : (block + 1) * rows, :], weight, start, tile
        )
        term[:, here] = term_of(attended[:rows, :], weight, start, tile)


def kept_terms(attended, weight):
    depth, width = weight.shape
    rows = attended.shape[0] // 4
    inside = pl.BlockSpec(memory_space=VMEM)
    return pl.pallas_call(
        kept_body,
        in_specs=[inside] * 2,
        out_specs=[inside] * 2,
        out_shape=[jax.ShapeDtypeStruct((rows, width), BF16)] * 2,
        compiler_params=params(12),
        cost_estimate=cost(8 * rows * depth * width, 4 * rows * width),
    )(attended, resident(weight))


def block_body(block, blocks, attended, weight, out):
    rows = attended.shape[0] // blocks
    for start in range(0, weight.shape[1], 512):
        out[:, start : start + 512] = term_of(
            attended[block * rows : (block + 1) * rows, :], weight, start, 512
        )


def block_term(attended, weight, block, blocks):
    depth, width = weight.shape
    rows = attended.shape[0] // blocks
    inside = pl.BlockSpec(memory_space=VMEM)
    return pl.pallas_call(
        functools.partial(block_body, block, blocks),
        in_specs=[inside] * 2,
        out_specs=inside,
        out_shape=jax.ShapeDtypeStruct((rows, width), BF16),
        compiler_params=params(12),
        cost_estimate=cost(2 * rows * depth * width, 2 * rows * width),
    )(attended, resident(weight))


def finish_body(token, term, near_x, near_y, far_y, far_x, *rest):
    out = rest[-1]

    def add(near, far):
        mixed = term[...].astype(F32) + near[...].astype(F32) + far[...].astype(F32)
        out[...] = (token[...].astype(F32) + mixed).astype(BF16)

    @pl.when(pl.program_id(0) == 0)
    def _():
        add(near_x, far_y)

    @pl.when(pl.program_id(0) == 1)
    def _():
        add(near_y, far_x)


def finish(token, term, near_x, near_y, far_y, far_x, before, part, parts):
    rows, width = token.shape
    span = width // 2 // parts
    tile = min(span, 1024)
    steps = span // tile
    half = width // 2 // tile

    def whole(h, j):
        return (0, h * half + part * steps + j)

    low = pl.BlockSpec((rows, tile), lambda h, j: (0, jnp.where(h == 0, j, steps - 1)))
    high = pl.BlockSpec((rows, tile), lambda h, j: (0, jnp.where(h == 0, 0, j)))
    specs = [pl.BlockSpec((rows, tile), whole)] * 2 + [low, high, low, high]
    operands = [token, term, near_x, near_y, far_y, far_x]
    aliases = {}
    if before is not None:
        specs.append(pl.BlockSpec(memory_space=ANY))
        operands.append(before)
        aliases = {6: 0}
    return pl.pallas_call(
        finish_body,
        grid=(2, steps),
        in_specs=specs,
        out_specs=pl.BlockSpec((rows, tile), whole),
        out_shape=jax.ShapeDtypeStruct((rows, width), BF16),
        input_output_aliases=aliases,
        compiler_params=params(40),
        cost_estimate=cost(rows * span, 20 * rows * span),
    )(*operands)


def on_device(
    tokens,
    norm_gain,
    w_query,
    query_scale,
    w_key,
    key_scale,
    w_value,
    value_scale,
    w_out,
    out_scale,
    score_vec,
    doc_ids,
    span_of,
):
    rows, width = tokens.shape
    half = width // 2
    n_ctx = lax.axis_size("ctx")
    n_tp = lax.axis_size("tp")
    length = n_tp * rows
    slot = lax.axis_index("ctx")
    member = lax.axis_index("tp")
    span_pos = span_of[slot]

    def flip_tp(value, flip):
        return lax.ppermute(value, "tp", [(i, i ^ flip) for i in range(n_tp)])

    query_cols, key_cols = w_query.shape[1], w_key.shape[1]
    kv_heads = key_cols // HDIM
    group = query_cols // key_cols
    gain = norm_gain[None, :]

    doc_iota = jnp.arange(NDOC, dtype=jnp.int32)
    counts = jnp.sum((doc_ids[None, :] == doc_iota[:, None]).astype(jnp.int32), 1)
    starts = jnp.sum(jnp.where(doc_iota[None, :] < doc_iota[:, None], counts[None, :], 0), 1)
    row_iota = jnp.arange(length, dtype=jnp.int32)
    position = span_pos * length + (member ^ (row_iota // rows)) * rows + row_iota % rows
    begun = starts[None, :] <= position[:, None]
    document = jnp.sum(begun.astype(jnp.int32), 1) - 1
    relative = position - jnp.max(jnp.where(begun, starts[None, :], 0), 1)
    frequency = 500000.0 ** (-2.0 * jnp.arange(HDIM // 2).astype(F32) / HDIM)
    angles = relative.astype(F32)[:, None] * frequency[None, :]
    cosine, sine = jnp.cos(angles), jnp.sin(angles)
    cosine = jnp.concatenate([cosine, cosine], 1)
    sine = jnp.concatenate([-sine, sine], 1)

    def exchange_along(value):
        return [value] + [
            lax.ppermute(value, "ctx", [(i, (i + 2 * step) % n_ctx) for i in range(n_ctx)])
            for step in range(1, n_ctx // 2)
        ]

    def exchange_across(held):
        return held + [
            lax.ppermute(one, "ctx", [(i, i ^ 1) for i in range(n_ctx)]) for one in held
        ]

    sources = [(slot - 2 * step) % n_ctx for step in range(n_ctx // 2)]
    sources += [((slot ^ 1) - 2 * step) % n_ctx for step in range(n_ctx // 2)]
    meta = jnp.concatenate(
        [
            span_pos[None],
            starts,
            member[None].astype(jnp.int32),
            jnp.take(span_of, jnp.stack(sources)),
        ]
    ).astype(jnp.int32)

    square = n_tp == 4
    if square:
        kinds = ((0,), (1, 2), (3,))
    else:
        kinds = ((0,),) + tuple((i, i + 1) for i in range(1, n_tp - 1, 2)) + ((n_tp - 1,),)
    tables = [
        tuple(
            one[flips[0] * rows : (flips[-1] + 1) * rows] for one in (cosine, sine)
        )
        for flips in kinds
    ]
    token_score = jnp.dot(tokens, score_vec, preferred_element_type=F32)
    vector = score_vec.astype(F32)[None, :]
    gain, tables, token_score, vector, meta, document, counts = lax.optimization_barrier(
        (gain, tables, token_score, vector, meta, document, counts)
    )
    near = {flip: flip_tp(tokens, flip) for flip in ((1, 2) if square else range(1, n_tp))}

    weight = dequant_joint((w_key, w_value, w_query), (key_scale, value_scale, query_scale))
    normed, own_pair = project_keys(
        [(tokens, 0), (tokens, 1)], rows, gain, weight, key_cols, *tables[0]
    )
    held = exchange_across(exchange_along(own_pair))
    own_query = project_queries(normed, weight, 2 * key_cols, *tables[0])

    if square:
        near[1], near[2], held = lax.optimization_barrier((near[1], near[2], held))
        low, high = halves(near[1], near[2])
        far_low, far_high = flip_tp(low, 2), flip_tp(high, 1)
    queries = [own_query]
    waiting = []
    for flips, table in zip(kinds[1:], tables[1:]):
        if square and flips == (3,):
            far_low, far_high, queries = lax.optimization_barrier((far_low, far_high, queries))
            parts = [(far_low, 0), (far_high, 0)]
        else:
            parts = [(near[flip], side) for flip in flips for side in range(2)]
        normed, pair = project_keys(parts, rows, gain, weight, key_cols, *table)
        waiting.append(exchange_along(pair))
        queries.append(project_queries(normed, weight, 2 * key_cols, *table))
    queries, late_scale = lax.optimization_barrier((queries, out_scale))
    back = dequant_back(w_out, late_scale)
    waiting, queries, back = lax.optimization_barrier((waiting, queries, back))
    for along in waiting:
        held += exchange_across(along)

    attended = attend(meta, queries, held, n_ctx, rows, kv_heads, group, kinds)

    def all_sum(value, axis, size, step):
        while step < size:
            value = value + lax.ppermute(value, axis, [(i, i ^ step) for i in range(size)])
            step *= 2
        return value

    def span_sums(attended, toward):
        row_score = jnp.sum(attended.astype(F32) * toward[:, 0][None, :], 1)
        row_score = row_score + jnp.concatenate([token_score, jnp.zeros((length - rows,), F32)])
        own = document[:, None] == doc_iota[None, :]
        partial = jnp.sum(jnp.where(own, row_score[:, None], 0.0), 0)
        return all_sum(partial, "ctx", n_ctx, 1)

    if not square:
        partial = span_sums(attended, toward_score(back, vector))
        mixed = block_term(attended, back, 0, n_tp).astype(F32)
        for flip in range(1, n_tp):
            mixed = mixed + flip_tp(block_term(attended, back, flip, n_tp), flip).astype(F32)
        totals = all_sum(partial, "tp", n_tp, 1)
        return ((tokens.astype(F32) + mixed).astype(BF16), totals / counts.astype(F32))

    parts = 2
    span = half // parts
    sent = []
    for part in range(parts):
        out_x, out_y = outward(attended, back, part * span, span)
        sent.append((flip_tp(out_x, 1), flip_tp(out_y, 2)))
        attended, vector, out_x, out_y = lax.optimization_barrier(
            (attended, vector, out_x, out_y)
        )
    inner, term = kept_terms(attended, back)
    partial = span_sums(attended, toward_score(back, vector))

    def onward(got, start):
        ours = inner[:, start : start + span].astype(F32)
        return (ours + got[rows:].astype(F32)).astype(BF16)

    hidden = None
    for part in range(parts):
        near_x, near_y = sent[part]
        near_x, near_y, inner, term, partial = lax.optimization_barrier(
            (near_x, near_y, inner, term, partial)
        )
        on_y, on_x = onward(near_x, part * span), onward(near_y, half + part * span)
        far_y, far_x = flip_tp(on_y, 2), flip_tp(on_x, 1)
        if part < 2:
            partial, on_y, on_x = lax.optimization_barrier((partial, on_y, on_x))
            partial = partial + flip_tp(partial, 1 + part)
        hidden = finish(tokens, term, near_x, near_y, far_y, far_x, hidden, part, parts)
    return (hidden, partial / counts.astype(F32))


def solution(mesh):
    return jax.shard_map(
        on_device,
        mesh=mesh,
        in_specs=(
            P(("ctx", "tp"), None),
            P(),
            P(None, "tp"),
            P(None, "tp"),
            P(None, "tp"),
            P(None, "tp"),
            P(None, "tp"),
            P(None, "tp"),
            P("tp", None),
            P("tp", None),
            P(),
            P(),
            P(),
        ),
        out_specs=(P(("ctx", "tp"), None), P()),
        check_vma=False,
    )
```

```python
import functools

import jax
import jax.numpy as jnp
from jax import lax
from jax.experimental import pallas as pl
from jax.experimental.pallas import tpu as pltpu
from jax.sharding import PartitionSpec as P

HDIM = 128
BLOCK = 128
NDOC = 4
F32 = jnp.float32
BF16 = jnp.bfloat16
ANY = pl.ANY
HBM = pltpu.HBM
VMEM = pltpu.VMEM
SMEM = pltpu.SMEM
MIB = 1 << 20


def params(mib):
    return pltpu.CompilerParams(vmem_limit_bytes=mib * MIB)


def cost(flops, moved):
    return pl.CostEstimate(flops=int(flops), bytes_accessed=int(moved), transcendentals=0)


def turn(values, cosine, sine):
    pieces = []
    for head in range(values.shape[1] // HDIM):
        one = values[:, head * HDIM : (head + 1) * HDIM]
        pieces.append(one * cosine + pltpu.roll(one, HDIM // 2, 1) * sine)
    return jnp.concatenate(pieces, 1)


def resident(value):
    return pltpu.with_memory_space_constraint(value, VMEM)


def outside(value):
    return pltpu.with_memory_space_constraint(value, HBM)


def normalize(parts, gain, normed):
    rows, half = parts[0].shape
    step, wide = 16, 1024
    for block in range(len(parts) // 2):
        pair = parts[2 * block : 2 * block + 2]

        @pl.loop(0, rows // step)
        def _(i):
            here = pl.ds(pl.multiple_of(i * step, step), step)
            there = pl.ds(pl.multiple_of(block * rows + i * step, step), step)
            square = jnp.zeros((step, wide), F32)
            for part in pair:
                for c in range(half // wide):
                    chunk = part[here, c * wide : (c + 1) * wide].astype(F32)
                    square = square + chunk * chunk
            factor = lax.rsqrt(jnp.sum(square, -1, keepdims=True) / (2 * half) + 1e-05)
            for side, part in enumerate(pair):
                for c in range(half // wide):
                    columns = slice(c * wide, (c + 1) * wide)
                    at = slice(side * half + c * wide, side * half + (c + 1) * wide)
                    chunk = part[here, columns].astype(F32)
                    normed[there, at] = (chunk * factor * gain[:, at]).astype(BF16)


def keys_and_values(normed, weight, cosine, sine, pair):
    key_cols = pair.shape[1] // 2
    product = jnp.dot(normed[...], weight[:, :key_cols], preferred_element_type=F32)
    pair[:, :key_cols] = turn(product, cosine[...], sine[...]).astype(BF16)
    product = jnp.dot(
        normed[...], weight[:, key_cols : 2 * key_cols], preferred_element_type=F32
    )
    pair[:, key_cols:] = product.astype(BF16)


def queries_of(normed, weight, skip, cosine, sine, query):
    tile = 2 * HDIM
    for start in range(0, query.shape[1], tile):
        product = jnp.dot(
            normed[...], weight[:, skip + start : skip + start + tile], preferred_element_type=F32
        )
        query[:, start : start + tile] = turn(product, cosine[...], sine[...]).astype(BF16)


def joint_body(count, *refs):
    stored, scales = refs[:count], refs[count : 2 * count]
    weight = refs[2 * count]
    slots, sems = refs[2 * count + 1 : 3 * count + 1], refs[3 * count + 1]
    depth = slots[0].shape[1]
    steps = weight.shape[0] // depth

    def fetch(i, slot):
        here = pl.ds(pl.multiple_of(i * depth, depth), depth)
        return [
            pltpu.make_async_copy(stored[n].at[here], slots[n].at[slot], sems.at[n, slot])
            for n in range(count)
        ]

    for copy in fetch(0, 0):
        copy.start()

    @pl.loop(0, steps)
    def _(i):
        slot = lax.rem(i, 2)

        @pl.when(i + 1 < steps)
        def _():
            for copy in fetch(i + 1, 1 - slot):
                copy.start()

        for copy in fetch(i, slot):
            copy.wait()
        for r in range(depth // BLOCK):
            out_rows = pl.ds(pl.multiple_of(i * depth + r * BLOCK, BLOCK), BLOCK)
            column = 0
            for n in range(count):
                for j in range(slots[n].shape[2] // BLOCK):
                    tile = slots[n][
                        slot, r * BLOCK : (r + 1) * BLOCK, j * BLOCK : (j + 1) * BLOCK
                    ].astype(F32)
                    factor = scales[n][i * (depth // BLOCK) + r, j]
                    weight[out_rows, column + j * BLOCK : column + (j + 1) * BLOCK] = (
                        tile * factor
                    ).astype(BF16)
                column += slots[n].shape[2]


def dequant_joint(stored, scales):
    width, depth = stored[0].shape[0], 512
    widths = [one.shape[1] for one in stored]
    return pl.pallas_call(
        functools.partial(joint_body, len(stored)),
        in_specs=[pl.BlockSpec(memory_space=HBM) for _ in widths]
        + [pl.BlockSpec(memory_space=SMEM) for _ in widths],
        out_specs=pl.BlockSpec(memory_space=VMEM),
        out_shape=VMEM((width, sum(widths)), BF16),
        scratch_shapes=[VMEM((2, depth, one), BF16) for one in widths]
        + [pltpu.SemaphoreType.DMA((len(widths), 2))],
        compiler_params=params(6),
        cost_estimate=cost(600 * width * sum(widths), 2 * width * sum(widths)),
    )(*[outside(one) for one in stored], *scales)


def keys_body(blocks, *refs):
    parts = refs[: 2 * blocks]
    gain, weight, cosine, sine, normed, pair = refs[2 * blocks :]
    normalize(parts, gain, normed)
    keys_and_values(normed, weight, cosine, sine, pair)


def project_keys(parts, rows, gain, weight, key_cols, cosine, sine):
    blocks = len(parts) // 2
    width = weight.shape[0]
    half, total = width // 2, rows * blocks
    inside = pl.BlockSpec(memory_space=VMEM)
    return pl.pallas_call(
        functools.partial(keys_body, blocks),
        grid=(1,),
        in_specs=[pl.BlockSpec((rows, half), lambda k, at=at: (0, at)) for _, at in parts]
        + [pl.BlockSpec((1, width), lambda k: (0, 0)), inside, inside, inside],
        out_specs=[pl.BlockSpec((total, width), lambda k: (0, 0)), inside],
        out_shape=[
            jax.ShapeDtypeStruct((total, width), BF16),
            jax.ShapeDtypeStruct((total, 2 * key_cols), BF16),
        ],
        compiler_params=params(6),
        cost_estimate=cost(8 * total * width * key_cols, 6 * total * width),
    )(*[one for one, _ in parts], gain, resident(weight), cosine, sine)


def queries_body(skip, normed, weight, cosine, sine, query):
    queries_of(normed, weight, skip, cosine, sine, query)


def project_queries(normed, weight, skip, cosine, sine):
    total, width = normed.shape
    columns = weight.shape[1] - skip
    inside = pl.BlockSpec(memory_space=VMEM)
    return pl.pallas_call(
        functools.partial(queries_body, skip),
        in_specs=[inside] * 4,
        out_specs=inside,
        out_shape=jax.ShapeDtypeStruct((total, columns), BF16),
        compiler_params=params(6),
        cost_estimate=cost(4 * total * width * columns, 4 * total * width),
    )(normed, resident(weight), cosine, sine)


def back_body(stored, scales, out, slots, sems):
    depth, width = slots.shape[1:]
    steps = stored.shape[0] // depth

    def fetch(i, slot):
        here = pl.ds(pl.multiple_of(i * depth, depth), depth)
        return pltpu.make_async_copy(stored.at[here], slots.at[slot], sems.at[slot])

    fetch(0, 0).start()

    @pl.loop(0, steps)
    def _(i):
        slot = lax.rem(i, 2)

        @pl.when(i + 1 < steps)
        def _():
            fetch(i + 1, 1 - slot).start()

        fetch(i, slot).wait()
        here = pl.ds(pl.multiple_of(i * depth, depth), depth)
        for j in range(width // BLOCK):
            there = slice(j * BLOCK, (j + 1) * BLOCK)
            factor = scales[i * depth // BLOCK, j]
            out[here, there] = (slots[slot, :, there].astype(F32) * factor).astype(BF16)


def dequant_back(stored, scales):
    rows, width = stored.shape
    depth = BLOCK
    return pl.pallas_call(
        back_body,
        in_specs=[pl.BlockSpec(memory_space=HBM), pl.BlockSpec(memory_space=SMEM)],
        out_specs=pl.BlockSpec(memory_space=VMEM),
        out_shape=VMEM((rows, width), BF16),
        scratch_shapes=[VMEM((2, depth, width), BF16), pltpu.SemaphoreType.DMA((2,))],
        compiler_params=params(5),
        cost_estimate=cost(8 * rows * width, 2 * rows * width),
    )(outside(stored), scales)


def toward_body(weight, vector, toward):
    rows, width = weight.shape
    step = 32

    @pl.loop(0, rows // step)
    def _(i):
        here = pl.ds(pl.multiple_of(i * step, step), step)
        run = jnp.zeros((step, BLOCK), F32)
        for j in range(width // BLOCK):
            there = slice(j * BLOCK, (j + 1) * BLOCK)
            run = run + weight[here, there].astype(F32) * vector[:, there]
        toward[here, :] = jnp.broadcast_to(jnp.sum(run, 1, keepdims=True), (step, BLOCK))


def toward_score(weight, vector):
    rows, width = weight.shape
    inside = pl.BlockSpec(memory_space=VMEM)
    return pl.pallas_call(
        toward_body,
        in_specs=[inside] * 2,
        out_specs=inside,
        out_shape=jax.ShapeDtypeStruct((rows, BLOCK), F32),
        compiler_params=params(5),
        cost_estimate=cost(8 * rows * width, 2 * rows * width),
    )(resident(weight), vector)


def halves_body(one, two, low, high):
    low[...] = one[...]
    high[...] = two[...]


def halves(one, two):
    rows, width = one.shape
    steps = 4
    tile = width // 2 // steps
    first = pl.BlockSpec((rows, tile), lambda j: (0, j))
    second = pl.BlockSpec((rows, tile), lambda j: (0, steps + j))
    return pl.pallas_call(
        halves_body,
        grid=(steps,),
        in_specs=[first, second],
        out_specs=[first, first],
        out_shape=[jax.ShapeDtypeStruct((rows, width // 2), BF16)] * 2,
        compiler_params=params(5),
        cost_estimate=cost(0, 4 * rows * width),
    )(one, two)


def attend_body(sizes, *refs):
    units, rows, kv_heads, group, chunk, kinds = sizes
    meta = refs[0]
    many = len(kinds)
    queries = refs[1 : 1 + many]
    held = refs[1 + many : 1 + many + many * units]
    out, pool, asked, kv_sem, q_sem = refs[1 + many + many * units :]
    length = sum(len(flips) for flips in kinds) * rows
    key_cols = kv_heads * HDIM
    mine = meta[0]
    starts = [meta[1 + d] for d in range(NDOC)]
    member = meta[1 + NDOC]
    span_at = 2 + NDOC

    def doc_start(position):
        found = jnp.int32(0)
        for one in starts:
            found = jnp.where(one <= position, one, found)
        return found

    first_span = doc_start(mine * length) // length
    q_copies = [
        pltpu.make_async_copy(
            queries[i],
            asked.at[pl.ds(flips[0] * rows, len(flips) * rows)],
            q_sem.at[i],
        )
        for i, flips in enumerate(kinds)
    ]
    for copy in q_copies:
        copy.start()

    def copies(unit, go):
        span = meta[span_at + unit]

        @pl.when((span >= first_span) & (span <= mine))
        def _():
            count = 0
            for kind, flips in enumerate(kinds):
                source = held[kind * units + unit]
                for piece, flip in enumerate(flips):
                    place = pl.multiple_of(
                        span * length + (member ^ flip) * rows, BLOCK
                    )
                    copy = pltpu.make_async_copy(
                        source.at[pl.ds(piece * rows, rows)],
                        pool.at[pl.ds(place, rows)],
                        kv_sem.at[unit, count],
                    )
                    count += 1
                    if go:
                        copy.start()
                    else:
                        copy.wait()

    for unit in range(units):
        copies(unit, True)
    for copy in q_copies:
        copy.wait()
    for unit in range(units):
        copies(unit, False)

    factor = HDIM ** (-0.5) * 1.4426950408889634

    @pl.loop(0, length // BLOCK)
    def _(index):
        at = pl.multiple_of(index * BLOCK, BLOCK)
        flip = at // rows
        position = mine * length + (member ^ flip) * rows + at % rows
        low = doc_start(position) // chunk
        high = (position + BLOCK - 1) // chunk
        row_pos = position + lax.broadcasted_iota(jnp.int32, (BLOCK, chunk), 0)
        row_start = doc_start(row_pos)
        lane = lax.broadcasted_iota(jnp.int32, (BLOCK, chunk), 1)
        for head in range(kv_heads):
            query = jnp.concatenate(
                [
                    asked[
                        pl.ds(at, BLOCK),
                        (head * group + g) * HDIM : (head * group + g + 1) * HDIM,
                    ]
                    for g in range(group)
                ],
                0,
            )

            def one_chunk(c, state):
                peak, total, acc = state
                here = pl.ds(pl.multiple_of(c * chunk, chunk), chunk)
                key = pool[here, head * HDIM : (head + 1) * HDIM]
                value = pool[here, key_cols + head * HDIM : key_cols + (head + 1) * HDIM]
                scores = lax.dot_general(
                    query, key, (((1,), (1,)), ((), ())), preferred_element_type=F32
                )
                key_pos = lane + c * chunk
                seen = (key_pos <= row_pos) & (key_pos >= row_start)
                scores = jnp.where(
                    seen[None], scores.reshape(group, BLOCK, chunk) * factor, -1e30
                ).reshape(group * BLOCK, chunk)
                higher = jnp.maximum(peak, jnp.max(scores, -1, keepdims=True))
                weights = jnp.exp2(scores - higher)
                fading = jnp.exp2(peak - higher)
                total = total * fading + jnp.sum(weights, -1, keepdims=True)
                acc = acc * fading + jnp.dot(
                    weights.astype(BF16), value, preferred_element_type=F32
                )
                return higher, total, acc

            state = (
                jnp.full((group * BLOCK, 1), -1e30, F32),
                jnp.zeros((group * BLOCK, 1), F32),
                jnp.zeros((group * BLOCK, HDIM), F32),
            )
            peak, total, acc = lax.fori_loop(low, high + 1, one_chunk, state)
            result = (acc / total).astype(BF16)
            for g in range(group):
                out[
                    pl.ds(at, BLOCK), (head * group + g) * HDIM : (head * group + g + 1) * HDIM
                ] = result[g * BLOCK : (g + 1) * BLOCK]


def attend(meta, queries, held, units, rows, kv_heads, group, kinds):
    blocks = sum(len(flips) for flips in kinds)
    length = blocks * rows
    columns = kv_heads * group * HDIM
    chunk = 2 * BLOCK
    sizes = (units, rows, kv_heads, group, chunk, kinds)
    return pl.pallas_call(
        functools.partial(attend_body, sizes),
        in_specs=[pl.BlockSpec(memory_space=SMEM)]
        + [pl.BlockSpec(memory_space=ANY)] * (len(kinds) * (1 + units)),
        out_specs=pl.BlockSpec(memory_space=VMEM),
        out_shape=jax.ShapeDtypeStruct((length, columns), BF16),
        scratch_shapes=[
            VMEM((units * length, 2 * kv_heads * HDIM), BF16),
            VMEM((length, columns), BF16),
            pltpu.SemaphoreType.DMA((units, blocks)),
            pltpu.SemaphoreType.DMA((len(kinds),)),
        ],
        compiler_params=params(
            3 + 4 * (units * length * kv_heads * HDIM + length * columns) // MIB
        ),
        cost_estimate=cost(8 * length * columns * 1024, 8 * MIB),
    )(meta, *queries, *held)


def term_of(rows_of, weight, start, width):
    return jnp.dot(
        rows_of, weight[:, start : start + width], preferred_element_type=F32
    ).astype(BF16)


def outward_body(starts, attended, weight, xo, yo):
    rows = attended.shape[0] // 4
    tile = 512
    for start in range(0, xo.shape[1], tile):
        here = slice(start, start + tile)
        for block, place in ((1, 0), (3, rows)):
            xo[place : place + rows, here] = term_of(
                attended[block * rows : (block + 1) * rows, :], weight, starts[0] + start, tile
            )
        for block, place in ((2, 0), (3, rows)):
            yo[place : place + rows, here] = term_of(
                attended[block * rows : (block + 1) * rows, :], weight, starts[1] + start, tile
            )


def outward(attended, weight, start, span):
    depth, width = weight.shape
    rows = attended.shape[0] // 4
    inside = pl.BlockSpec(memory_space=VMEM)
    return pl.pallas_call(
        functools.partial(outward_body, (start, width // 2 + start)),
        in_specs=[inside] * 2,
        out_specs=[inside] * 2,
        out_shape=[jax.ShapeDtypeStruct((2 * rows, span), BF16)] * 2,
        compiler_params=params(12),
        cost_estimate=cost(16 * rows * depth * span, 8 * rows * span),
    )(attended, resident(weight))


def kept_body(attended, weight, inner, term):
    rows = attended.shape[0] // 4
    width = weight.shape[1]
    tile = 512
    for start in range(0, width, tile):
        here = slice(start, start + tile)
        block = 2 if start < width // 2 else 1
        inner[:, here] = term_of(
            attended[block * rows : (block + 1) * rows, :], weight, start, tile
        )
        term[:, here] = term_of(attended[:rows, :], weight, start, tile)


def kept_terms(attended, weight):
    depth, width = weight.shape
    rows = attended.shape[0] // 4
    inside = pl.BlockSpec(memory_space=VMEM)
    return pl.pallas_call(
        kept_body,
        in_specs=[inside] * 2,
        out_specs=[inside] * 2,
        out_shape=[jax.ShapeDtypeStruct((rows, width), BF16)] * 2,
        compiler_params=params(12),
        cost_estimate=cost(8 * rows * depth * width, 4 * rows * width),
    )(attended, resident(weight))


def block_body(block, blocks, attended, weight, out):
    rows = attended.shape[0] // blocks
    for start in range(0, weight.shape[1], 512):
        out[:, start : start + 512] = term_of(
            attended[block * rows : (block + 1) * rows, :], weight, start, 512
        )


def block_term(attended, weight, block, blocks):
    depth, width = weight.shape
    rows = attended.shape[0] // blocks
    inside = pl.BlockSpec(memory_space=VMEM)
    return pl.pallas_call(
        functools.partial(block_body, block, blocks),
        in_specs=[inside] * 2,
        out_specs=inside,
        out_shape=jax.ShapeDtypeStruct((rows, width), BF16),
        compiler_params=params(12),
        cost_estimate=cost(2 * rows * depth * width, 2 * rows * width),
    )(attended, resident(weight))


def finish_body(token, term, near_x, near_y, far_y, far_x, *rest):
    out = rest[-1]

    def add(near, far):
        mixed = term[...].astype(F32) + near[...].astype(F32) + far[...].astype(F32)
        out[...] = (token[...].astype(F32) + mixed).astype(BF16)

    @pl.when(pl.program_id(0) == 0)
    def _():
        add(near_x, far_y)

    @pl.when(pl.program_id(0) == 1)
    def _():
        add(near_y, far_x)


def finish(token, term, near_x, near_y, far_y, far_x, before, part, parts):
    rows, width = token.shape
    span = width // 2 // parts
    tile = min(span, 1024)
    steps = span // tile
    half = width // 2 // tile

    def whole(h, j):
        return (0, h * half + part * steps + j)

    low = pl.BlockSpec((rows, tile), lambda h, j: (0, jnp.where(h == 0, j, steps - 1)))
    high = pl.BlockSpec((rows, tile), lambda h, j: (0, jnp.where(h == 0, 0, j)))
    specs = [pl.BlockSpec((rows, tile), whole)] * 2 + [low, high, low, high]
    operands = [token, term, near_x, near_y, far_y, far_x]
    aliases = {}
    if before is not None:
        specs.append(pl.BlockSpec(memory_space=ANY))
        operands.append(before)
        aliases = {6: 0}
    return pl.pallas_call(
        finish_body,
        grid=(2, steps),
        in_specs=specs,
        out_specs=pl.BlockSpec((rows, tile), whole),
        out_shape=jax.ShapeDtypeStruct((rows, width), BF16),
        input_output_aliases=aliases,
        compiler_params=params(40),
        cost_estimate=cost(rows * span, 20 * rows * span),
    )(*operands)


def on_device(
    tokens,
    norm_gain,
    w_query,
    query_scale,
    w_key,
    key_scale,
    w_value,
    value_scale,
    w_out,
    out_scale,
    score_vec,
    doc_ids,
    span_of,
):
    rows, width = tokens.shape
    half = width // 2
    n_ctx = lax.axis_size("ctx")
    n_tp = lax.axis_size("tp")
    length = n_tp * rows
    slot = lax.axis_index("ctx")
    member = lax.axis_index("tp")
    span_pos = span_of[slot]

    def flip_tp(value, flip):
        return lax.ppermute(value, "tp", [(i, i ^ flip) for i in range(n_tp)])

    query_cols, key_cols = w_query.shape[1], w_key.shape[1]
    kv_heads = key_cols // HDIM
    group = query_cols // key_cols
    gain = norm_gain[None, :]

    doc_iota = jnp.arange(NDOC, dtype=jnp.int32)
    counts = jnp.sum((doc_ids[None, :] == doc_iota[:, None]).astype(jnp.int32), 1)
    starts = jnp.sum(jnp.where(doc_iota[None, :] < doc_iota[:, None], counts[None, :], 0), 1)
    row_iota = jnp.arange(length, dtype=jnp.int32)
    position = span_pos * length + (member ^ (row_iota // rows)) * rows + row_iota % rows
    begun = starts[None, :] <= position[:, None]
    document = jnp.sum(begun.astype(jnp.int32), 1) - 1
    relative = position - jnp.max(jnp.where(begun, starts[None, :], 0), 1)
    frequency = 500000.0 ** (-2.0 * jnp.arange(HDIM // 2).astype(F32) / HDIM)
    angles = relative.astype(F32)[:, None] * frequency[None, :]
    cosine, sine = jnp.cos(angles), jnp.sin(angles)
    cosine = jnp.concatenate([cosine, cosine], 1)
    sine = jnp.concatenate([-sine, sine], 1)

    def exchange_along(value):
        return [value] + [
            lax.ppermute(value, "ctx", [(i, (i + 2 * step) % n_ctx) for i in range(n_ctx)])
            for step in range(1, n_ctx // 2)
        ]

    def exchange_across(held):
        return held + [
            lax.ppermute(one, "ctx", [(i, i ^ 1) for i in range(n_ctx)]) for one in held
        ]

    sources = [(slot - 2 * step) % n_ctx for step in range(n_ctx // 2)]
    sources += [((slot ^ 1) - 2 * step) % n_ctx for step in range(n_ctx // 2)]
    meta = jnp.concatenate(
        [
            span_pos[None],
            starts,
            member[None].astype(jnp.int32),
            jnp.take(span_of, jnp.stack(sources)),
        ]
    ).astype(jnp.int32)

    square = n_tp == 4
    if square:
        kinds = ((0,), (1, 2), (3,))
    else:
        kinds = ((0,),) + tuple((i, i + 1) for i in range(1, n_tp - 1, 2)) + ((n_tp - 1,),)
    tables = [
        tuple(
            one[flips[0] * rows : (flips[-1] + 1) * rows] for one in (cosine, sine)
        )
        for flips in kinds
    ]
    token_score = jnp.dot(tokens, score_vec, preferred_element_type=F32)
    vector = score_vec.astype(F32)[None, :]
    gain, tables, token_score, vector, meta, document, counts = lax.optimization_barrier(
        (gain, tables, token_score, vector, meta, document, counts)
    )
    near = {flip: flip_tp(tokens, flip) for flip in ((1, 2) if square else range(1, n_tp))}

    weight = dequant_joint((w_key, w_value, w_query), (key_scale, value_scale, query_scale))
    normed, own_pair = project_keys(
        [(tokens, 0), (tokens, 1)], rows, gain, weight, key_cols, *tables[0]
    )
    held = exchange_across(exchange_along(own_pair))
    own_query = project_queries(normed, weight, 2 * key_cols, *tables[0])

    if square:
        near[1], near[2], held = lax.optimization_barrier((near[1], near[2], held))
        low, high = halves(near[1], near[2])
        far_low, far_high = flip_tp(low, 2), flip_tp(high, 1)
    queries = [own_query]
    waiting = []
    for flips, table in zip(kinds[1:], tables[1:]):
        if square and flips == (3,):
            far_low, far_high, queries = lax.optimization_barrier((far_low, far_high, queries))
            parts = [(far_low, 0), (far_high, 0)]
        else:
            parts = [(near[flip], side) for flip in flips for side in range(2)]
        normed, pair = project_keys(parts, rows, gain, weight, key_cols, *table)
        waiting.append(exchange_along(pair))
        queries.append(project_queries(normed, weight, 2 * key_cols, *table))
    queries, late_scale = lax.optimization_barrier((queries, out_scale))
    back = dequant_back(w_out, late_scale)
    waiting, queries, back = lax.optimization_barrier((waiting, queries, back))
    for along in waiting:
        held += exchange_across(along)

    attended = attend(meta, queries, held, n_ctx, rows, kv_heads, group, kinds)

    def all_sum(value, axis, size, step):
        while step < size:
            value = value + lax.ppermute(value, axis, [(i, i ^ step) for i in range(size)])
            step *= 2
        return value

    def span_sums(attended, toward):
        row_score = jnp.sum(attended.astype(F32) * toward[:, 0][None, :], 1)
        row_score = row_score + jnp.concatenate([token_score, jnp.zeros((length - rows,), F32)])
        own = document[:, None] == doc_iota[None, :]
        partial = jnp.sum(jnp.where(own, row_score[:, None], 0.0), 0)
        return all_sum(partial, "ctx", n_ctx, 1)

    if not square:
        partial = span_sums(attended, toward_score(back, vector))
        mixed = block_term(attended, back, 0, n_tp).astype(F32)
        for flip in range(1, n_tp):
            mixed = mixed + flip_tp(block_term(attended, back, flip, n_tp), flip).astype(F32)
        totals = all_sum(partial, "tp", n_tp, 1)
        return ((tokens.astype(F32) + mixed).astype(BF16), totals / counts.astype(F32))

    parts = 4
    span = half // parts
    sent = []
    for part in range(parts):
        out_x, out_y = outward(attended, back, part * span, span)
        sent.append((flip_tp(out_x, 1), flip_tp(out_y, 2)))
        attended, vector, out_x, out_y = lax.optimization_barrier(
            (attended, vector, out_x, out_y)
        )
    inner, term = kept_terms(attended, back)
    partial = span_sums(attended, toward_score(back, vector))

    def onward(got, start):
        ours = inner[:, start : start + span].astype(F32)
        return (ours + got[rows:].astype(F32)).astype(BF16)

    hidden = None
    for part in range(parts):
        near_x, near_y = sent[part]
        near_x, near_y, inner, term, partial = lax.optimization_barrier(
            (near_x, near_y, inner, term, partial)
        )
        on_y, on_x = onward(near_x, part * span), onward(near_y, half + part * span)
        far_y, far_x = flip_tp(on_y, 2), flip_tp(on_x, 1)
        if part < 2:
            partial, on_y, on_x = lax.optimization_barrier((partial, on_y, on_x))
            partial = partial + flip_tp(partial, 1 + part)
        hidden = finish(tokens, term, near_x, near_y, far_y, far_x, hidden, part, parts)
    return (hidden, partial / counts.astype(F32))


def solution(mesh):
    return jax.shard_map(
        on_device,
        mesh=mesh,
        in_specs=(
            P(("ctx", "tp"), None),
            P(),
            P(None, "tp"),
            P(None, "tp"),
            P(None, "tp"),
            P(None, "tp"),
            P(None, "tp"),
            P(None, "tp"),
            P("tp", None),
            P("tp", None),
            P(),
            P(),
            P(),
        ),
        out_specs=(P(("ctx", "tp"), None), P()),
        check_vma=False,
    )
```
